32 devices in a mesh: dp: 8 (over y, x, core), mp: 4 (over z).
Axes of the slice: x: 2, y: 2, z: 4, core: 2. Of those that a mesh axis runs over, the one named last changes fastest.
Arguments:
- queries: bfloat16 [5120, 4096], P('dp', 'mp'), may hold values from -180 to 180
- keys: bfloat16 [5120, 512], P('dp', 'mp'), may hold values from -6 to 6
- values: bfloat16 [5120, 512], P('dp', 'mp'), may hold values from -6 to 6
- prompt_keys: bfloat16 [128, 512], P(None, 'mp'), may hold values from -6 to 6
- prompt_values: bfloat16 [128, 512], P(None, 'mp'), may hold values from -6 to 6
- out_weight: bfloat16 [4096, 8192], P('mp', 'dp'), may hold values from -0.09375 to 0.09375
- out_grad: bfloat16 [5120, 8192], P('dp'), may hold values from -6 to 6
- lengths: int32 [8, 8], P('dp'), may hold values from 1 to 320, 640 in all within a row
Outputs:
- mixed: bfloat16 [5120, 8192], P('dp', 'mp')
- prompt_key_grad: float32 [128, 512], P('dp', 'mp')
- prompt_value_grad: float32 [128, 512], P('dp', 'mp')
The draws below stay inside these ranges and needn't reach their ends.
All inputs are finite; a program needn't handle non-finite values.
Results may differ from the reference program's by a relative error of at most 0.024.
Values may be sent and summed in bfloat16 or wider, within the bound.
No kernel may reach another device: no remote copies, remote signals or barrier semaphores. Data moves between devices by JAX's collectives and lax.ppermute only.
A program may use at most 192 MiB of HBM per device.

```python
import math
import jax
import jax.numpy as jnp
import numpy as np
from jax import lax

D = 8192
HEADS = 32
KV_HEADS = 4
HD = 128
PROMPT = 128
DOCS = 8
TOK_DEV = 640
DOC_MOST = 320
TOKENS = 5120
N_DP = 8
N_MP = 4


def drawn_pair(key):
    keys_f = jnp.clip(jax.random.normal(jax.random.fold_in(key, 11), (TOKENS, KV_HEADS * HD), jnp.float32), -6.0, 6.0)
    query_f = jnp.clip(jax.random.normal(jax.random.fold_in(key, 12), (TOKENS, HEADS * HD), jnp.float32), -6.0, 6.0)
    return (keys_f, query_f)


def draw_queries(key, part):
    return drawn_pair(key)[1].astype(jnp.bfloat16)


def draw_keys(key, part):
    return drawn_pair(key)[0].astype(jnp.bfloat16)


def steps_of(rng, extent, shards, smallest, top_value):
    gain, own = 1.0, jax.random.fold_in(rng, 6)
    for dim, shards_of in shards:
        steps = jnp.exp(jax.random.uniform(jax.random.fold_in(own, dim), (shards_of,), jnp.float32, smallest / len(shards), top_value / len(shards)))
        gain = gain * jnp.repeat(steps, extent[dim] // shards_of).reshape([-1 if axis == dim else 1 for axis in range(len(extent))])
    return gain


def length_profile(number_of, total, bound, skew):
    portions = [(1 << 20) // math.isqrt(rank ** skew) + 1 for rank in range(2, number_of + 1)]
    spare, holding = total - bound - (number_of - 1), [1] * (number_of - 1)
    while spare > 0:
        candidates = [i for i in range(number_of - 1) if holding[i] < bound]
        mass, left = sum([portions[i] for i in candidates]), spare
        for i in candidates:
            addition = min(bound - holding[i], max(1, left * portions[i] // mass), spare)
            holding[i] = holding[i] + addition
            spare = spare - addition
    return np.array([bound] + holding)


def ragged(key, number_of, total, limit, skew):
    if number_of == 2:
        one = jax.random.randint(key, (), max(1, total - limit), min(limit, total - 1) + 1)
        return jnp.stack([one, total - one])
    sizes = jnp.asarray(length_profile(number_of, total, limit, skew), jnp.int32)
    twos = (number_of - 1) // 2
    giver, sink = sizes[1:1 + 2 * twos:2], sizes[2:2 + 2 * twos:2]
    slack = jnp.minimum(giver - 1, limit - sink)
    passed = jax.random.randint(jax.random.fold_in(key, 1), (twos,), 0, 1 << 20) % (slack + 1)
    sizes = sizes.at[1:1 + 2 * twos:2].set(giver - passed).at[2:2 + 2 * twos:2].set(sink + passed)
    return sizes[jax.random.permutation(jax.random.fold_in(key, 2), number_of)]


def bell_draw(key, extent, spread, most, pieces=(), kind=jnp.bfloat16):
    array = spread * jax.random.normal(key, extent, jnp.float32)
    if pieces:
        array = array * steps_of(key, extent, pieces, -0.22, 0.18)
    return jnp.clip(array, -most, most).astype(kind)


def setup_inputs(seed: int = 0) -> dict:
    arg_keys = jax.random.split(jax.random.key(seed), 9)
    return {
        "queries": draw_queries(jax.random.fold_in(arg_keys[8], 71), 0),
        "keys": draw_keys(jax.random.fold_in(arg_keys[8], 71), 0),
        "values": bell_draw(arg_keys[2], (TOKENS, KV_HEADS * HD), 1.0, 6.0, ((0, 8), (1, 4))),
        "prompt_keys": bell_draw(arg_keys[3], (PROMPT, KV_HEADS * HD), 1.0, 6.0, ((1, 4),)),
        "prompt_values": bell_draw(arg_keys[4], (PROMPT, KV_HEADS * HD), 1.0, 6.0, ((1, 4),)),
        "out_weight": bell_draw(arg_keys[5], (HEADS * HD, D), (HEADS * HD) ** -0.5, 0.09375, ((0, 4), (1, 8))),
        "out_grad": bell_draw(arg_keys[6], (TOKENS, D), 1.0, 6.0, ((0, 8),)),
        "lengths": jax.vmap(lambda own: ragged(own, DOCS, TOK_DEV, DOC_MOST, 2))(jax.random.split(arg_keys[7], N_DP)).reshape((N_DP, DOCS)).astype(jnp.int32),
    }


rope_base = 1000000.0


def doc_layout(lens, count):
    ends = jnp.cumsum(lens).astype(jnp.int32)
    starts = ends - lens
    index = jnp.arange(count, dtype=jnp.int32)
    segment = jnp.sum((index[:, None] >= ends[None, :]).astype(jnp.int32), axis=1).astype(jnp.int32)
    doc_ids = jnp.arange(lens.shape[0], dtype=jnp.int32)
    offset = jnp.sum(jnp.where(segment[:, None] == doc_ids[None, :], starts[None, :], 0), axis=1).astype(jnp.int32)
    return segment, index - offset


def rotate(field, position):
    half = HD // 2
    freq = rope_base ** (-2.0 * jnp.arange(half, dtype=jnp.float32) / HD)
    angle = position.astype(jnp.float32)[:, None] * freq[None, :]
    cosine = jnp.cos(angle)[:, None, :]
    sine = jnp.sin(angle)[:, None, :]
    first = field[..., :half].astype(jnp.float32)
    second = field[..., half:].astype(jnp.float32)
    return jnp.concatenate([first * cosine - second * sine, second * cosine + first * sine], axis=-1).astype(jnp.bfloat16)


def block_work(queries, keys, values, prompt_keys, prompt_values, out_weight, out_grad, lens):
    tok_rows = queries.shape[0]
    groups = HEADS // KV_HEADS
    scale = HD ** -0.5
    segment, position = doc_layout(lens, tok_rows)
    q_rot = rotate(queries.reshape(tok_rows, HEADS, HD), position).reshape(tok_rows, KV_HEADS, groups, HD)
    k_rot = rotate(keys.reshape(tok_rows, KV_HEADS, HD), position)
    key_all = jnp.concatenate([prompt_keys.reshape(PROMPT, KV_HEADS, HD), k_rot], axis=0)
    value_all = jnp.concatenate([prompt_values.reshape(PROMPT, KV_HEADS, HD), values.reshape(tok_rows, KV_HEADS, HD)], axis=0)
    index = jnp.arange(tok_rows, dtype=jnp.int32)
    own = (segment[:, None] == segment[None, :]) & (index[None, :] <= index[:, None])
    key_mask = jnp.concatenate([jnp.ones((tok_rows, PROMPT), dtype=bool), own], axis=1)
    scores = jnp.einsum('tkgd,skd->kgts', q_rot.astype(jnp.float32), key_all.astype(jnp.float32)) * scale
    scores = jnp.where(key_mask[None, None], scores, -1e30)
    shifted = jnp.exp(scores - jnp.max(scores, axis=-1, keepdims=True))
    shifted = jnp.where(key_mask[None, None], shifted, 0.0)
    probs = shifted / jnp.sum(shifted, axis=-1, keepdims=True)
    probs_b = probs.astype(jnp.bfloat16)
    attn = jnp.einsum('kgts,skd->tkgd', probs_b.astype(jnp.float32), value_all.astype(jnp.float32))
    attn = attn.astype(jnp.bfloat16).reshape(tok_rows, HEADS * HD)
    width = (HEADS // N_MP) * HD
    total = jnp.zeros((tok_rows, D), jnp.float32)
    for member in range(N_MP):
        partial_value = jnp.dot(attn[:, member * width:(member + 1) * width], out_weight[member * width:(member + 1) * width], preferred_element_type=jnp.float32)
        partial_value = lax.optimization_barrier(partial_value.astype(jnp.bfloat16))
        total = total + partial_value.astype(jnp.float32)
    mixed = total.astype(jnp.bfloat16)
    grad_attn = jnp.dot(out_grad, out_weight.T, preferred_element_type=jnp.float32).astype(jnp.bfloat16)
    grad_attn = grad_attn.reshape(tok_rows, KV_HEADS, groups, HD)
    value_grad = jnp.einsum('kgts,tkgd->skd', probs_b[..., :PROMPT].astype(jnp.float32), grad_attn.astype(jnp.float32))
    grad_probs = jnp.einsum('tkgd,skd->kgts', grad_attn.astype(jnp.float32), value_all.astype(jnp.float32))
    d_scores = probs * (grad_probs - jnp.sum(probs * grad_probs, axis=-1, keepdims=True)) * scale
    d_scores = d_scores.astype(jnp.bfloat16)
    key_grad = jnp.einsum('kgts,tkgd->skd', d_scores[..., :PROMPT].astype(jnp.float32), q_rot.astype(jnp.float32))
    return mixed, key_grad.reshape(PROMPT, KV_HEADS * HD), value_grad.reshape(PROMPT, KV_HEADS * HD)


def reference(queries, keys, values, prompt_keys, prompt_values, out_weight, out_grad, lengths):
    def one_block(block):
        start = (block * TOK_DEV).astype(jnp.int32)
        return block_work(
            lax.dynamic_slice_in_dim(queries, start, TOK_DEV, 0),
            lax.dynamic_slice_in_dim(keys, start, TOK_DEV, 0),
            lax.dynamic_slice_in_dim(values, start, TOK_DEV, 0),
            prompt_keys, prompt_values, out_weight,
            lax.dynamic_slice_in_dim(out_grad, start, TOK_DEV, 0),
            lengths[block])

    mixed, key_grad, value_grad = lax.map(one_block, jnp.arange(N_DP, dtype=jnp.int32))
    return mixed.reshape(TOKENS, D), jnp.sum(key_grad, axis=0), jnp.sum(value_grad, axis=0)
```

```python
import functools
import math

import jax
import jax.numpy as jnp
from jax import lax
from jax.experimental import pallas as pl
from jax.experimental.pallas import tpu as pltpu
from jax.sharding import PartitionSpec as P

HD = 128
rope_base = 1000000.0
F32 = jnp.float32
BF16 = jnp.bfloat16
VMEM_LIMIT = 60 * 1024 * 1024


def doc_layout(lens, count):
    ends = jnp.cumsum(lens)
    starts = ends - lens
    index = jnp.arange(count, dtype=jnp.int32)
    segment = jnp.sum((index[:, None] >= ends[None, :]).astype(jnp.int32), axis=1)
    doc_ids = jnp.arange(lens.shape[0], dtype=jnp.int32)
    offset = jnp.sum(jnp.where(segment[:, None] == doc_ids[None, :], starts[None, :], 0), axis=1)
    return offset, index - offset


def rope_tables(position):
    half = HD // 2
    freq = rope_base ** (-2.0 * jnp.arange(half, dtype=F32) / HD)
    angle = position.astype(F32)[:, None] * freq[None, :]
    cosine = jnp.cos(angle)
    sine = jnp.sin(angle)
    return (
        jnp.concatenate([cosine, cosine], axis=-1),
        jnp.concatenate([-sine, sine], axis=-1),
    )


def nt(a, b):
    return lax.dot_general(a, b, (((1,), (1,)), ((), ())), preferred_element_type=F32)


def tn(a, b):
    return lax.dot_general(a, b, (((0,), (0,)), ((), ())), preferred_element_type=F32)


def attn_body(
    blocks, per, c2, q_ref, k_ref, v_ref, pk_ref, pv_ref, cos_ref, sin_ref, start_ref,
    attn_ref, o_ref, p_ref, qr_ref, kall, vall, bias,
):
    step = pl.program_id(0)
    rows = q_ref.shape[0]
    slices = o_ref.shape[0]
    prompt = pk_ref.shape[0]
    base = pl.multiple_of(step * rows, rows)

    def rot(x):
        return (x * cos_ref[...] + pltpu.roll(x, HD // 2, 1) * sin_ref[...]).astype(BF16)

    kall[pl.ds(base, rows), :] = rot(k_ref[...].astype(F32))
    vall[pl.ds(base, rows), :] = v_ref[...]

    def block(number):
        width = (number + 1) * rows
        col = lax.broadcasted_iota(jnp.int32, (rows, width), 1)
        row = lax.broadcasted_iota(jnp.int32, (rows, width), 0) + number * rows
        seen = (col >= start_ref[...]) & (col <= row)
        bias[:, :width] = jnp.where(seen, 0.0, -1e30)

        @pl.loop(0, slices)
        def _(s):
            for h in range(per):
                lane = pl.multiple_of((s * per + h) * HD, HD)
                qr = rot(q_ref[:, pl.ds(lane, HD)].astype(F32))
                qr_ref[s, :, h * HD : (h + 1) * HD] = qr
                sp = nt(qr, pk_ref[...])
                st = nt(qr, kall[:width, :]) + bias[:, :width]
                top = jnp.maximum(
                    jnp.max(sp, axis=-1, keepdims=True), jnp.max(st, axis=-1, keepdims=True)
                )
                ep = jnp.exp2((sp - top) * c2)
                et = jnp.exp2((st - top) * c2)
                total = jnp.sum(ep, axis=-1, keepdims=True) + jnp.sum(et, axis=-1, keepdims=True)
                inv = 1.0 / total
                o = jnp.dot(ep.astype(BF16), pv_ref[...], preferred_element_type=F32)
                o += jnp.dot(et.astype(BF16), vall[:width, :], preferred_element_type=F32)
                o = o * inv
                o_ref[s, :, h * HD : (h + 1) * HD] = o
                attn_ref[:, pl.ds(lane, HD)] = o.astype(BF16)
                p_ref[s, :, h * prompt : (h + 1) * prompt] = (ep * inv).astype(BF16)

    for number in range(blocks):
        pl.when(step == number)(functools.partial(block, number))


def attention(queries, keys, values, pk, pv, cosine, sine, start, slices):
    tok, width = queries.shape
    prompt = pk.shape[0]
    per = width // HD // slices
    rows = 128 if tok % 128 == 0 else tok
    blocks = tok // rows
    c2 = HD ** (-0.5) * math.log2(math.e)
    cells = tok * (width // HD) * (prompt + tok * (blocks + 1) // (2 * blocks))
    whole = lambda shape: pl.BlockSpec(shape, lambda i: (0,) * len(shape))
    tile = lambda cols: pl.BlockSpec((rows, cols), lambda i: (i, 0))
    stack = lambda cols: pl.BlockSpec((slices, rows, cols), lambda i: (0, i, 0))
    return pl.pallas_call(
        functools.partial(attn_body, blocks, per, c2),
        grid=(blocks,),
        in_specs=[
            tile(width), tile(HD), tile(HD), whole((prompt, HD)), whole((prompt, HD)),
            tile(HD), tile(HD), tile(1),
        ],
        out_specs=[tile(width), stack(per * HD), stack(per * prompt), stack(per * HD)],
        out_shape=[
            jax.ShapeDtypeStruct((tok, width), BF16),
            jax.ShapeDtypeStruct((slices, tok, per * HD), F32),
            jax.ShapeDtypeStruct((slices, tok, per * prompt), BF16),
            jax.ShapeDtypeStruct((slices, tok, per * HD), BF16),
        ],
        scratch_shapes=[
            pltpu.VMEM((tok, HD), BF16),
            pltpu.VMEM((tok, HD), BF16),
            pltpu.VMEM((rows, tok), F32),
        ],
        compiler_params=pltpu.CompilerParams(dimension_semantics=("arbitrary",)),
        cost_estimate=pl.CostEstimate(
            flops=4 * cells * HD, transcendentals=cells, bytes_accessed=12 * tok * width
        ),
        name="attn_fwd",
    )(queries, keys, values, pk, pv, cosine, sine, start)


def grad_body(
    count, per, scale, idx_ref, og_ref, o_ref, p_ref, qr_ref, pv_ref, kv_ref, *rest
):
    w_refs = rest[:count]
    out_ref, ogbuf, wbuf, obuf, pbuf, qbuf, acc, sems = rest[count:]
    halves, srows = wbuf.shape[1], wbuf.shape[2]
    cols = wbuf.shape[3]
    tok = ogbuf.shape[1]
    sel = idx_ref[0]

    def og_copy(n, block):
        src = og_ref.at[:, pl.ds(pl.multiple_of(block * cols, cols), cols)]
        return pltpu.make_async_copy(src, ogbuf.at[n], sems.at[n])

    for n in range(count):
        og_copy(n, idx_ref[1 + n]).start()
        pltpu.make_async_copy(w_refs[n], wbuf.at[n], sems.at[n]).start()
    extra = []
    for h in range(halves):
        for src, dst in ((o_ref, obuf), (p_ref, pbuf), (qr_ref, qbuf)):
            extra.append(pltpu.make_async_copy(src.at[2 * h + sel], dst.at[h], sems.at[count]))
    for copy in extra:
        copy.start()

    rt = tok // 2 if tok % 32 == 0 else tok

    @pl.loop(0, count)
    def _(n):
        og_copy(n, 0).wait()
        pltpu.make_async_copy(w_refs[0], wbuf.at[n], sems.at[n]).wait()

        @pl.loop(0, tok // rt)
        def _(t):
            rows = pl.ds(pl.multiple_of(t * rt, rt), rt)
            for h in range(halves):
                part = nt(ogbuf[n, rows, :], wbuf[n, h])
                c = slice(h * srows, (h + 1) * srows)

                @pl.when(n == 0)
                def _():
                    acc[rows, c] = part

                @pl.when(n > 0)
                def _():
                    acc[rows, c] += part

    for copy in extra:
        copy.wait()
    prompt = pv_ref.shape[0]
    out_ref[...] = kv_ref[...]
    for h in range(halves):
        for k in range(per):
            g = acc[:, h * srows + k * HD : h * srows + (k + 1) * HD].astype(BF16)
            o = obuf[h, :, k * HD : (k + 1) * HD]
            p = pbuf[h, :, k * prompt : (k + 1) * prompt]
            qr = qbuf[h, :, k * HD : (k + 1) * HD]
            delta = jnp.sum(g.astype(F32) * o, axis=-1, keepdims=True)
            gp = nt(g, pv_ref[...])
            d = (p.astype(F32) * (gp - delta) * scale).astype(BF16)
            out_ref[:, :HD] += tn(d, qr)
            out_ref[:, HD:] += tn(p, g)


def grad_part(idx, out_grad, o, p, qr, pv, kv, parts):
    count = len(parts)
    halves, srows, cols = parts[0].shape
    tok = out_grad.shape[0]
    prompt = pv.shape[0]
    per = srows // HD
    anyspec = pl.BlockSpec(memory_space=pl.ANY)
    vmem = pl.BlockSpec(memory_space=pltpu.VMEM)
    return pl.pallas_call(
        functools.partial(grad_body, count, per, HD ** (-0.5)),
        in_specs=[pl.BlockSpec(memory_space=pltpu.SMEM)] + [anyspec] * 4 + [vmem] * 2
        + [anyspec] * count,
        out_specs=vmem,
        out_shape=jax.ShapeDtypeStruct((prompt, 2 * HD), F32),
        scratch_shapes=[
            pltpu.VMEM((count, tok, cols), BF16),
            pltpu.VMEM((count, halves, srows, cols), BF16),
            pltpu.VMEM((halves, tok, srows), F32),
            pltpu.VMEM((halves, tok, per * prompt), BF16),
            pltpu.VMEM((halves, tok, srows), BF16),
            pltpu.VMEM((tok, halves * srows), F32),
            pltpu.SemaphoreType.DMA((count + 1,)),
        ],
        compiler_params=pltpu.CompilerParams(vmem_limit_bytes=VMEM_LIMIT),
        cost_estimate=pl.CostEstimate(
            flops=2 * tok * halves * srows * cols * count,
            transcendentals=0,
            bytes_accessed=2 * count * cols * (tok + halves * srows) + 8 * tok * halves * srows,
        ),
        name="grad_part",
    )(idx, out_grad, o, p, qr, pv, kv, *parts)


def mixed_body(sources, has_acc, last, idx_ref, *rest):
    total = 1 + max(
        max(e[0] for e in attn + weight) for attn, weight in sources
    )
    refs = rest[:total]
    rest = rest[total:]
    if has_acc:
        acc_in, rest = rest[0], rest[1:]
    out_ref, abuf, wbuf, acc, sems = rest
    for s, (attn, weight) in enumerate(sources):
        for ref, cond in attn:
            copy = pltpu.make_async_copy(refs[ref], abuf.at[s], sems.at[s])
            if cond is None:
                copy.start()
            else:
                pl.when(idx_ref[cond] == 1)(copy.start)
        for ref, sub, cond, r, c, h, w in weight:
            rows = pl.ds(pl.multiple_of(idx_ref[r], h), h)
            cols = pl.ds(pl.multiple_of(idx_ref[c], w), w)
            src = refs[ref] if sub is None else refs[ref].at[sub]
            copy = pltpu.make_async_copy(src, wbuf.at[s, rows, cols], sems.at[s])
            if cond is None:
                copy.start()
            else:
                pl.when(idx_ref[cond] == 1)(copy.start)
    if has_acc:
        first = pltpu.make_async_copy(acc_in, acc, sems.at[len(sources)])
        first.start()
        first.wait()
    tok, width = acc.shape
    ct = 256 if width % 256 == 0 else width
    rt = tok // 2 if tok % 32 == 0 else tok
    for s in range(len(sources)):
        attn, weight = sources[s]
        pltpu.make_async_copy(refs[attn[0][0]], abuf.at[s], sems.at[s]).wait()
        pltpu.make_async_copy(wbuf.at[s], wbuf.at[s], sems.at[s]).wait()

        @pl.loop(0, width // ct)
        def _(c):
            cols = pl.ds(pl.multiple_of(c * ct, ct), ct)
            for t in range(tok // rt):
                rows = slice(t * rt, (t + 1) * rt)
                part = jnp.dot(abuf[s, rows, :], wbuf[s, :, cols], preferred_element_type=F32)
                if s > 0 or has_acc:
                    part = acc[rows, cols] + part
                if s == len(sources) - 1:
                    out_ref[rows, cols] = part.astype(out_ref.dtype)
                else:
                    acc[rows, cols] = part


def mixed_part(idx, sources, operands, acc, last, tok, depth, width):
    count = len(sources)
    anyspec = pl.BlockSpec(memory_space=pl.ANY)
    extra = [] if acc is None else [acc]
    return pl.pallas_call(
        functools.partial(mixed_body, sources, acc is not None, last),
        in_specs=[pl.BlockSpec(memory_space=pltpu.SMEM)]
        + [anyspec] * (len(operands) + len(extra)),
        out_specs=pl.BlockSpec(memory_space=pltpu.VMEM),
        out_shape=jax.ShapeDtypeStruct((tok, width), BF16 if last else F32),
        scratch_shapes=[
            pltpu.VMEM((count, tok, depth), BF16),
            pltpu.VMEM((count, depth, width), BF16),
            pltpu.VMEM((tok, width), F32),
            pltpu.SemaphoreType.DMA((count + 1,)),
        ],
        compiler_params=pltpu.CompilerParams(vmem_limit_bytes=VMEM_LIMIT),
        cost_estimate=pl.CostEstimate(
            flops=2 * tok * depth * width * count,
            transcendentals=0,
            bytes_accessed=2 * count * depth * (tok + width) + 6 * tok * width,
        ),
        name="mixed_last" if last else "mixed_part",
    )(idx, *operands, *extra)


def after(value, *others):
    return lax.optimization_barrier((value,) + others)[0]


def per_device(
    n_dp, n_mp, queries, keys, values, prompt_keys, prompt_values, out_weight, out_grad, lengths
):
    tok = queries.shape[0]
    depth, cb = out_weight.shape
    width = out_grad.shape[1] // n_mp
    rs = depth // n_mp
    ring = n_dp // n_mp
    p = lax.axis_index("dp")
    m = lax.axis_index("mp")
    q, lane = p // ring, p % ring
    par, hi = q & 1, q >> 1

    def dp_xor(bits, value):
        return lax.ppermute(value, "dp", [(i, i ^ bits) for i in range(n_dp)])

    def mp_pairs(pairs, value):
        return lax.ppermute(value, "mp", pairs)

    X, Y = ring, 2 * ring
    sides = range(1, ring)

    w4 = out_weight.reshape(2, 2, rs, cb)
    even = lax.dynamic_index_in_dim(w4, par, 1, keepdims=False)
    odd = lax.dynamic_index_in_dim(w4, 1 - par, 1, keepdims=False)
    x_a = dp_xor(X, odd)
    y_a = dp_xor(Y, even)
    d_a = dp_xor(Y, x_a)
    d_b = dp_xor(X, y_a)
    x_b = dp_xor(X, after(even, d_b))
    y_b = dp_xor(Y, after(odd, d_a))
    a_parts = [even, x_a, y_a, d_a]
    b_parts = [odd, x_b, y_b, d_b]

    start, position = doc_layout(lengths[0], tok)
    cosine, sine = rope_tables(position)
    attn, o, probs, q_rot = attention(
        queries, keys, values, prompt_keys, prompt_values, cosine, sine, start[:, None], n_mp
    )

    swap = [(i, i ^ 1) for i in range(n_mp)]
    middle = [(1, 2), (2, 1)]
    outward = [(1, 0), (2, 3)]
    a1 = mp_pairs(swap, attn)
    b1 = mp_pairs(middle, attn)
    b2 = mp_pairs(middle, a1)
    c1 = mp_pairs(outward, b1)
    c2 = mp_pairs(outward, b2)

    mine = [lax.dynamic_index_in_dim(part, hi, 0, keepdims=False) for part in a_parts]

    def piece(k):
        return lax.select_n(q ^ m ^ k, *mine)

    def over(k, value):
        return mp_pairs([(i, i ^ k) for i in range(n_mp)], value)

    g1 = over(1, piece(1))
    g2 = over(2, piece(2))
    p3 = piece(3)
    g3a = over(3, p3[: rs // 2])
    g3b = over(3, p3[rs // 2 :])
    x1, y1 = dp_xor(X, g1), dp_xor(Y, g1)
    d1 = dp_xor(Y, x1)
    x2, y2 = dp_xor(X, g2), dp_xor(Y, g2)
    d2 = dp_xor(X, y2)
    x3a, y3a = dp_xor(X, g3a), dp_xor(Y, g3a)
    x3b, y3b = dp_xor(X, g3b), dp_xor(Y, g3b)
    d3a = dp_xor(Y, x3a)
    d3b = dp_xor(X, y3b)

    def spread(value):
        return [value] + [dp_xor(side, value) for side in sides]

    a_all = [spread(part) for part in a_parts]
    b_all = [spread(part) for part in b_parts]

    order = [(j, side) for side in range(ring) for j in range(n_mp)]
    blocks = [(q ^ j) * ring + (lane ^ side) for j, side in order]

    def grads(kv, parts, sel):
        idx = jnp.stack([sel] + blocks).astype(jnp.int32)
        return grad_part(
            idx, out_grad, o, probs, q_rot, prompt_values, kv,
            [parts[j][side] for j, side in order],
        )

    kv = jnp.zeros((prompt_values.shape[0], 2 * HD), F32)
    kv = grads(kv, a_all, par)
    kv = grads(kv, b_all, 1 - par)
    bit = n_dp // 2
    while bit:
        half = kv.shape[0] // 2
        low, high = kv[:half], kv[half:]
        upper = (p & bit) != 0
        kv = jnp.where(upper, high, low) + dp_xor(bit, jnp.where(upper, low, high))
        bit //= 2

    idx, place = [], {}

    def at(key, value):
        if key not in place:
            place[key] = len(idx)
            idx.append(jnp.asarray(value, jnp.int32))
        return place[key]

    operands = []

    def operand(value):
        operands.append(value)
        return len(operands) - 1

    def column(side):
        return at(("col", side), (lane ^ side) * cb)

    def row(j, offset=0):
        return at(("row", j, offset), (q ^ j) * rs + offset)

    own_w = []
    for j in range(n_mp):
        for sel, parts in ((par, a_all), (1 - par, b_all)):
            tag = "a" if parts is a_all else "b"
            for side in range(ring):
                ref = operand(parts[j][side])
                for h in range(2):
                    own_w.append((
                        ref,
                        h,
                        at(("own", j), (q ^ m) == j),
                        at(("ownrow", tag, h), (2 * h + sel) * rs),
                        column(side), rs, cb,
                    ))
    sources = [([(operand(attn), None)], own_w)]

    def foreign(entries):
        out = []
        for j, offset, value in entries:
            for side, part in enumerate(spread(value)):
                out.append((
                    operand(part), None, None, row(j, offset), column(side), value.shape[0], cb
                ))
        return out

    mid = at("mid", (m == 1) | (m == 2))
    end = at("end", (m == 0) | (m == 3))
    sources.append(
        ([(operand(a1), None)], foreign([(0, 0, g1), (1, 0, x1), (2, 0, y1), (3, 0, d1)]))
    )
    sources.append((
        [(operand(b2), mid), (operand(c1), end)],
        foreign([(0, 0, g2), (1, 0, x2), (2, 0, y2), (3, 0, d2)]),
    ))
    lower = rs // 2
    cut = len(operands)
    last = (
        [(operand(b1), mid), (operand(c2), end)],
        foreign([
            (0, 0, g3a), (1, 0, x3a), (2, 0, y3a), (3, 0, d3a),
            (0, lower, g3b), (1, lower, x3b), (2, lower, y3b), (3, lower, d3b),
        ]),
    )
    shifted = tuple([(e[0] - cut,) + tuple(e[1:]) for e in part] for part in last)
    table = jnp.stack(idx)
    acc = mixed_part(table, sources, operands[:cut], None, False, tok, depth, width)
    mixed = mixed_part(table, [shifted], operands[cut:], acc, True, tok, depth, width)
    return mixed, kv[:, :HD], kv[:, HD:]


def solution(mesh):
    n_dp, n_mp = mesh.shape["dp"], mesh.shape["mp"]
    in_specs = (
        P("dp", "mp"),
        P("dp", "mp"),
        P("dp", "mp"),
        P(None, "mp"),
        P(None, "mp"),
        P("mp", "dp"),
        P("dp", None),
        P("dp", None),
    )
    out_specs = (P("dp", "mp"), P("dp", "mp"), P("dp", "mp"))
    return jax.shard_map(
        functools.partial(per_device, n_dp, n_mp),
        mesh=mesh, in_specs=in_specs, out_specs=out_specs, check_vma=False,
    )
```

```python
import functools
import math

import jax
import jax.numpy as jnp
from jax import lax
from jax.experimental import pallas as pl
from jax.experimental.pallas import tpu as pltpu
from jax.sharding import PartitionSpec as P

HD = 128
rope_base = 1000000.0
F32 = jnp.float32
BF16 = jnp.bfloat16
VMEM_LIMIT = 60 * 1024 * 1024


def nt(a, b):
    return lax.dot_general(a, b, (((1,), (1,)), ((), ())), preferred_element_type=F32)


def tn(a, b):
    return lax.dot_general(a, b, (((0,), (0,)), ((), ())), preferred_element_type=F32)


def attn_body(
    blocks, per, scale2, lens_ref, q_ref, k_ref, v_ref, pk_ref, pv_ref, freq_ref,
    attn_ref, o_ref, p_ref, qr_ref, kall, vall, bias,
):
    step = pl.program_id(0)
    rows = q_ref.shape[0]
    slices = o_ref.shape[0]
    prompt = pk_ref.shape[0]
    base = step * rows
    here = pl.multiple_of(prompt + base, math.gcd(prompt, rows))

    row = lax.broadcasted_iota(jnp.int32, (rows, HD), 0) + base
    col = lax.broadcasted_iota(jnp.int32, (rows, HD), 1)
    start = jnp.zeros((rows, HD), jnp.int32)
    end = jnp.int32(0)
    for doc in range(lens_ref.shape[1]):
        start = jnp.where(row >= end, end, start)
        end = end + lens_ref[0, doc]
    angle = (row - start).astype(F32) * freq_ref[...]
    cosine = jnp.cos(angle)
    sine = jnp.sin(angle)
    sine = jnp.where(col < HD // 2, -sine, sine)

    def rot(x):
        return (x * cosine + pltpu.roll(x, HD // 2, 1) * sine).astype(BF16)

    @pl.when(step == 0)
    def _():
        kall[:prompt, :] = pk_ref[...]
        vall[:prompt, :HD] = pv_ref[...]
        vall[:, HD:] = jnp.ones((vall.shape[0], HD), BF16)

    kall[pl.ds(here, rows), :] = rot(k_ref[...].astype(F32))
    vall[pl.ds(here, rows), :HD] = v_ref[...]

    def block(number):
        width = (number + 1) * rows
        for b in range(0, width, HD):
            key = col + b
            seen = (key >= start) & (key <= row)
            bias[:, b : b + HD] = jnp.where(seen, 0.0, -1e30)
        for head in range(slices * per):
            s, h = head // per, head % per
            lane = slice(head * HD, (head + 1) * HD)
            mine = slice(h * HD, (h + 1) * HD)
            qr = rot(q_ref[:, lane].astype(F32))
            qr_ref[s, :, mine] = qr
            sc = nt(qr, kall[: prompt + width, :])
            sp = sc[:, :prompt]
            st = sc[:, prompt:] + bias[:, :width]
            top = jnp.maximum(
                jnp.max(sp, axis=-1, keepdims=True), jnp.max(st, axis=-1, keepdims=True)
            )
            ep = jnp.exp2((sp - top) * scale2)
            et = jnp.exp2((st - top) * scale2)
            e = jnp.concatenate([ep.astype(BF16), et.astype(BF16)], axis=1)
            both = jnp.dot(e, vall[: prompt + width, :], preferred_element_type=F32)
            inv = 1.0 / both[:, HD:]
            o = both[:, :HD] * inv
            o_ref[s, :, mine] = o
            attn_ref[:, lane] = o.astype(BF16)
            p_ref[s, :, h * prompt : (h + 1) * prompt] = (
                ep * (inv if prompt == HD else inv[:, :1])
            ).astype(BF16)

    for number in range(blocks):
        pl.when(step == number)(functools.partial(block, number))


def attention(queries, keys, values, pk, pv, lengths, slices):
    tok, width = queries.shape
    prompt = pk.shape[0]
    per = width // HD // slices
    rows = HD if tok % HD == 0 else tok
    blocks = tok // rows
    scale2 = HD ** (-0.5) * math.log2(math.e)
    cells = tok * (width // HD) * (prompt + tok * (blocks + 1) // (2 * blocks))
    freq = rope_base ** (-2.0 * jnp.arange(HD // 2, dtype=F32) / HD)
    freq = jnp.concatenate([freq, freq])[None, :]
    whole = lambda shape: pl.BlockSpec(shape, lambda i: (0,) * len(shape))
    tile = lambda cols: pl.BlockSpec((rows, cols), lambda i: (i, 0))
    stack = lambda cols: pl.BlockSpec((slices, rows, cols), lambda i: (0, i, 0))
    return pl.pallas_call(
        functools.partial(attn_body, blocks, per, scale2),
        grid=(blocks,),
        in_specs=[
            pl.BlockSpec(memory_space=pltpu.SMEM),
            tile(width), tile(HD), tile(HD), whole((prompt, HD)), whole((prompt, HD)),
            whole((1, HD)),
        ],
        out_specs=[tile(width), stack(per * HD), stack(per * prompt), stack(per * HD)],
        out_shape=[
            jax.ShapeDtypeStruct((tok, width), BF16),
            jax.ShapeDtypeStruct((slices, tok, per * HD), F32),
            jax.ShapeDtypeStruct((slices, tok, per * prompt), BF16),
            jax.ShapeDtypeStruct((slices, tok, per * HD), BF16),
        ],
        scratch_shapes=[
            pltpu.VMEM((prompt + tok, HD), BF16),
            pltpu.VMEM((prompt + tok, 2 * HD), BF16),
            pltpu.VMEM((rows, tok), F32),
        ],
        compiler_params=pltpu.CompilerParams(dimension_semantics=("arbitrary",)),
        cost_estimate=pl.CostEstimate(
            flops=4 * cells * HD, transcendentals=cells, bytes_accessed=12 * tok * width
        ),
        name="attn_fwd",
    )(lengths, queries, keys, values, pk, pv, freq)


def grad_body(
    kinds, per, scale, idx_ref, og_ref, o_ref, p_ref, qr_ref, pv_ref, kv_ref, *rest
):
    count = len(kinds)
    w_refs = rest[:count]
    out_ref, ogbuf, wbuf, obuf, pbuf, qbuf, acc, sems = rest[count:]
    cols = wbuf.shape[2]
    halves, tok, srows = obuf.shape
    sel = idx_ref[0]

    def og_copy(n, block):
        src = og_ref.at[:, pl.ds(pl.multiple_of(block * cols, cols), cols)]
        return pltpu.make_async_copy(src, ogbuf.at[n], sems.at[n])

    for n in range(count):
        og_copy(n, idx_ref[1 + n]).start()
        for h in range(halves):
            src = w_refs[n].at[h, sel] if kinds[n] else w_refs[n].at[h]
            dst = wbuf.at[n, pl.ds(h * srows, srows)]
            pltpu.make_async_copy(src, dst, sems.at[n]).start()
    extra = []
    for h in range(halves):
        for src, dst in ((o_ref, obuf), (p_ref, pbuf), (qr_ref, qbuf)):
            extra.append(pltpu.make_async_copy(src.at[2 * h + sel], dst.at[h], sems.at[count]))
    for copy in extra:
        copy.start()

    @pl.loop(0, count)
    def _(n):
        og_copy(n, 0).wait()
        pltpu.make_async_copy(wbuf.at[n], wbuf.at[n], sems.at[n]).wait()

        @pl.when(n == 0)
        def _():
            acc[...] = nt(ogbuf[n], wbuf[n])

        @pl.when(n > 0)
        def _():
            acc[...] += nt(ogbuf[n], wbuf[n])

    for copy in extra:
        copy.wait()
    prompt = pv_ref.shape[0]
    out_ref[...] = kv_ref[...]
    for h in range(halves):
        for k in range(per):
            g = acc[:, h * srows + k * HD : h * srows + (k + 1) * HD].astype(BF16)
            o = obuf[h, :, k * HD : (k + 1) * HD]
            p = pbuf[h, :, k * prompt : (k + 1) * prompt]
            qr = qbuf[h, :, k * HD : (k + 1) * HD]
            delta = jnp.sum(g.astype(F32) * o, axis=-1, keepdims=True)
            gp = nt(g, pv_ref[...])
            d = (p.astype(F32) * (gp - delta) * scale).astype(BF16)
            out_ref[:, :HD] += tn(d, qr)
            out_ref[:, HD:] += tn(p, g)


def grad_part(idx, out_grad, o, p, qr, pv, kv, parts):
    count = len(parts)
    kinds = tuple(part.ndim == 4 for part in parts)
    halves, (srows, cols) = 2, parts[0].shape[-2:]
    tok = out_grad.shape[0]
    prompt = pv.shape[0]
    per = srows // HD
    anyspec = pl.BlockSpec(memory_space=pl.ANY)
    vmem = pl.BlockSpec(memory_space=pltpu.VMEM)
    return pl.pallas_call(
        functools.partial(grad_body, kinds, per, HD ** (-0.5)),
        in_specs=[pl.BlockSpec(memory_space=pltpu.SMEM)] + [anyspec] * 4 + [vmem] * 2
        + [anyspec] * count,
        out_specs=vmem,
        out_shape=jax.ShapeDtypeStruct((prompt, 2 * HD), F32),
        scratch_shapes=[
            pltpu.VMEM((count, tok, cols), BF16),
            pltpu.VMEM((count, halves * srows, cols), BF16),
            pltpu.VMEM((halves, tok, srows), F32),
            pltpu.VMEM((halves, tok, per * prompt), BF16),
            pltpu.VMEM((halves, tok, srows), BF16),
            pltpu.VMEM((tok, halves * srows), F32),
            pltpu.SemaphoreType.DMA((count + 1,)),
        ],
        compiler_params=pltpu.CompilerParams(vmem_limit_bytes=VMEM_LIMIT),
        cost_estimate=pl.CostEstimate(
            flops=2 * tok * halves * srows * cols * count,
            transcendentals=0,
            bytes_accessed=2 * count * cols * (tok + halves * srows) + 8 * tok * halves * srows,
        ),
        name="grad_part",
    )(idx, out_grad, o, p, qr, pv, kv, *parts)


def mixed_body(sources, total, cb, has_acc, idx_ref, *rest):
    refs = rest[:total]
    rest = rest[total:]
    if has_acc:
        acc_ref, rest = rest[0], rest[1:]
    out_ref, abuf, wbuf, asem, wsem = rest
    step = pl.program_id(0)
    ct = out_ref.shape[1]

    def begin(copy, cond):
        if cond is None:
            copy.start()
        else:
            pl.when(idx_ref[cond] == 1)(copy.start)

    @pl.when(step == 0)
    def _():
        for s, (attn, weight) in enumerate(sources):
            for ref, cond in attn:
                begin(pltpu.make_async_copy(refs[ref], abuf.at[s], asem.at[s]), cond)
            for ref, sub, cond, r, c, h in weight:
                src = refs[ref] if sub is None else refs[ref].at[sub]
                block = idx_ref[c]
                rows = pl.ds(pl.multiple_of(idx_ref[r], h), h)
                cols = pl.ds(pl.multiple_of(block * cb, cb), cb)
                dst = wbuf.at[s, rows, cols]
                begin(pltpu.make_async_copy(src, dst, wsem.at[s, block]), cond)

    part = acc_ref[...] if has_acc else None
    tiles = cb // ct
    block = step // tiles
    for s in range(len(sources)):
        attn = sources[s][0]

        @pl.when(step == 0)
        def _():
            pltpu.make_async_copy(refs[attn[0][0]], abuf.at[s], asem.at[s]).wait()

        @pl.when(step % tiles == 0)
        def _():
            view = wbuf.at[s, :, pl.ds(pl.multiple_of(block * cb, cb), cb)]
            pltpu.make_async_copy(view, view, wsem.at[s, block]).wait()

        cols = pl.ds(pl.multiple_of(step * ct, ct), ct)
        new = jnp.dot(abuf[s], wbuf[s, :, cols], preferred_element_type=F32)
        part = new if part is None else part + new
    out_ref[...] = part.astype(out_ref.dtype)


def mixed_part(idx, sources, operands, acc, dtype, tok, depth, width, cb):
    count = len(sources)
    ct = 512 if cb % 512 == 0 else cb
    anyspec = pl.BlockSpec(memory_space=pl.ANY)
    tile = pl.BlockSpec((tok, ct), lambda c: (0, c))
    extra = [] if acc is None else [acc]
    return pl.pallas_call(
        functools.partial(mixed_body, sources, len(operands), cb, acc is not None),
        grid=(width // ct,),
        in_specs=[pl.BlockSpec(memory_space=pltpu.SMEM)]
        + [anyspec] * len(operands) + [tile] * len(extra),
        out_specs=tile,
        out_shape=jax.ShapeDtypeStruct((tok, width), dtype),
        scratch_shapes=[
            pltpu.VMEM((count, tok, depth), BF16),
            pltpu.VMEM((count, depth, width), BF16),
            pltpu.SemaphoreType.DMA((count,)),
            pltpu.SemaphoreType.DMA((count, width // cb)),
        ],
        compiler_params=pltpu.CompilerParams(
            dimension_semantics=("arbitrary",), vmem_limit_bytes=VMEM_LIMIT
        ),
        cost_estimate=pl.CostEstimate(
            flops=2 * tok * depth * width * count,
            transcendentals=0,
            bytes_accessed=2 * count * depth * (tok + width) + 6 * tok * width,
        ),
        name="mixed_part" if acc is None else "mixed_last",
    )(idx, *operands, *extra)


def after(value, *others):
    return lax.optimization_barrier((value,) + others)[0]


def per_device(
    n_dp, n_mp, queries, keys, values, prompt_keys, prompt_values, out_weight, out_grad, lengths
):
    tok = queries.shape[0]
    depth, cb = out_weight.shape
    width = out_grad.shape[1] // n_mp
    rs = depth // n_mp
    ring = n_dp // n_mp
    p = lax.axis_index("dp")
    m = lax.axis_index("mp")
    q, lane = p // ring, p % ring
    par, hi = q & 1, q >> 1

    def dp_xor(bits, value):
        return lax.ppermute(value, "dp", [(i, i ^ bits) for i in range(n_dp)])

    def mp_pairs(pairs, value):
        return lax.ppermute(value, "mp", pairs)

    X, Y = ring, 2 * ring
    sides = range(1, ring)

    w4 = out_weight.reshape(2, 2, rs, cb)
    even = lax.dynamic_index_in_dim(w4, par, 1, keepdims=False)
    odd = lax.dynamic_index_in_dim(w4, 1 - par, 1, keepdims=False)
    x_a = dp_xor(X, odd)
    y_a = dp_xor(Y, even)

    attn, o, probs, q_rot = attention(
        queries, keys, values, prompt_keys, prompt_values, lengths, n_mp
    )
    swap = [(i, i ^ 1) for i in range(n_mp)]
    middle = [(1, 2), (2, 1)]
    outward = [(1, 0), (2, 3)]
    a1 = mp_pairs(swap, attn)
    b1 = mp_pairs(middle, attn)

    d_a = dp_xor(Y, after(x_a, attn))
    d_b = dp_xor(X, after(y_a, attn))
    x_b = dp_xor(X, after(even, d_b))
    y_b = dp_xor(Y, after(odd, d_a))
    a_parts = [x_a, y_a, d_a]
    b_parts = [x_b, y_b, d_b]

    mine = [
        lax.dynamic_index_in_dim(part, hi, 0, keepdims=False) for part in [even] + a_parts
    ]

    def piece(k):
        return lax.select_n(q ^ m ^ k, *mine)

    def over(k, value):
        return mp_pairs([(i, i ^ k) for i in range(n_mp)], value)

    g1 = over(1, piece(1))
    g2 = over(2, piece(2))
    g3 = over(3, after(piece(3), g1))
    b2 = mp_pairs(middle, after(a1, g1))
    c1 = mp_pairs(outward, after(b1, g1))
    c2 = mp_pairs(outward, after(b2, c1))

    lower = rs // 2
    g12 = jnp.stack([g1, g2])
    x12, y12 = dp_xor(X, after(g12, x_b)), dp_xor(Y, after(g12, y_b))
    d1 = dp_xor(Y, x12[0])
    d2 = dp_xor(X, y12[1])
    x3, y3 = dp_xor(X, after(g3, x12)), dp_xor(Y, after(g3, y12))
    d3a = dp_xor(Y, x3[:lower])
    d3b = dp_xor(X, y3[lower:])

    def spread(value):
        return [value] + [dp_xor(side, value) for side in sides]

    own_all = spread(w4)
    a_all = [own_all] + [spread(part) for part in a_parts]
    b_all = [own_all] + [spread(part) for part in b_parts]

    order = [(j, side) for side in range(ring) for j in range(n_mp)]
    blocks = [(q ^ j) * ring + (lane ^ side) for j, side in order]

    def grads(kv, parts, sel):
        idx = jnp.stack([sel] + blocks).astype(jnp.int32)
        return grad_part(
            idx, out_grad, o, probs, q_rot, prompt_values, kv,
            [parts[j][side] for j, side in order],
        )

    kv = jnp.zeros((prompt_values.shape[0], 2 * HD), F32)
    kv = grads(kv, a_all, par)
    kv = grads(kv, b_all, 1 - par)
    bit = n_dp // 2
    while bit:
        half = kv.shape[0] // 2
        low, high = kv[:half], kv[half:]
        upper = (p & bit) != 0
        kv = jnp.where(upper, high, low) + dp_xor(bit, jnp.where(upper, low, high))
        bit //= 2

    idx, place = [], {}

    def at(key, value):
        if key not in place:
            place[key] = len(idx)
            idx.append(jnp.asarray(value, jnp.int32))
        return place[key]

    class Call:
        def __init__(self):
            self.operands, self.sources = [], []

        def operand(self, value):
            for number, known in enumerate(self.operands):
                if known is value:
                    return number
            self.operands.append(value)
            return len(self.operands) - 1

        def add(self, attns, weights):
            self.sources.append((
                [(self.operand(value), cond) for value, cond in attns],
                [(self.operand(entry[0]),) + entry[1:] for entry in weights],
            ))

        def run(self, table, acc, dtype):
            return mixed_part(
                table, self.sources, self.operands, acc, dtype, tok, depth, width, cb
            )

    def column(side):
        return at(("col", side), lane ^ side)

    def row(j, offset=0):
        return at(("row", j, offset), (q ^ j) * rs + offset)

    own_w = []
    for j in range(n_mp):
        cond = at(("own", j), (q ^ m) == j)
        for side in range(ring):
            if j == 0:
                for h in range(2):
                    for low in range(2):
                        slot = at(("full", h, low), (2 * h + low) * rs)
                        own_w.append((own_all[side], (h, low), cond, slot, column(side), rs))
                continue
            for tag, sel, parts in (("a", par, a_all), ("b", 1 - par, b_all)):
                for h in range(2):
                    slot = at((tag, h), (2 * h + sel) * rs)
                    own_w.append((parts[j][side], h, cond, slot, column(side), rs))

    def foreign(entries):
        out = []
        for value, pieces in entries:
            for side, part in enumerate(spread(value)):
                for sub, j, offset, rows in pieces:
                    out.append((part, sub, None, row(j, offset), column(side), rows))
        return out

    pair = [g12, x12, y12]
    mid = at("mid", (m == 1) | (m == 2))
    end = at("end", (m == 0) | (m == 3))
    pair_all = [spread(value) for value in pair]

    def paired(k, diagonal):
        out = foreign([(diagonal, [(None, 3, 0, rs)])])
        for j, parts in enumerate(pair_all):
            for side, part in enumerate(parts):
                out.append((part, k, None, row(j), column(side), rs))
        return out

    first = Call()
    first.add([(attn, None)], own_w)
    first.add([(a1, None)], paired(0, d1))
    first.add([(b2, mid), (c1, end)], paired(1, d2))
    final = Call()
    final.add(
        [(b1, mid), (c2, end)],
        foreign([
            (g3, [(None, 0, 0, rs)]), (x3, [(None, 1, 0, rs)]), (y3, [(None, 2, 0, rs)]),
            (d3a, [(None, 3, 0, lower)]), (d3b, [(None, 3, lower, lower)]),
        ]),
    )
    table = jnp.stack(idx)
    acc = first.run(table, None, F32)
    mixed = final.run(table, acc, BF16)
    return mixed, kv[:, :HD], kv[:, HD:]


def solution(mesh):
    n_dp, n_mp = mesh.shape["dp"], mesh.shape["mp"]
    in_specs = (
        P("dp", "mp"),
        P("dp", "mp"),
        P("dp", "mp"),
        P(None, "mp"),
        P(None, "mp"),
        P("mp", "dp"),
        P("dp", None),
        P("dp", None),
    )
    out_specs = (P("dp", "mp"), P("dp", "mp"), P("dp", "mp"))
    return jax.shard_map(
        functools.partial(per_device, n_dp, n_mp),
        mesh=mesh, in_specs=in_specs, out_specs=out_specs, check_vma=False,
    )
```
